32 devices in a mesh: space: 4 (over y, x), orb: 8 (over z, core).
Axes of the slice: x: 2, y: 2, z: 4, core: 2. Of those that a mesh axis runs over, the one named last changes fastest.
Arguments:
- orbitals: float32 [16, 16, 32, 1024], P('space', None, None, 'orb'), may hold values from -6 to 6
- potential: float32 [16, 16, 32], P('space'), may hold values from 0 to 2
Outputs:
- updated: float32 [16, 16, 32, 1024], P('space', None, None, 'orb')
The draws below stay inside these ranges and needn't reach their ends.
All inputs are finite; a program needn't handle non-finite values.
Results may differ from the reference program's by a relative error of at most 0.00007.
Values sent between devices are 32-bit elements; how exact they have to be, the bound alone decides.
A program may use at most 64 MiB of HBM per device.

```python
import jax
import jax.numpy as jnp
from jax import lax

NY = 16
NZ = 32
ORB_DEV = 128
PANEL = 512
DEGREE = 4
NX = 16
ORBS = 1024
PANEL_DEV = 64
N_ORB = 8


def levels(own_key, dims, split, low, largest):
    def one(dim, parts):
        steps = jax.random.uniform(jax.random.fold_in(jax.random.fold_in(own_key, 6), dim), (parts,), jnp.float32, low / len(split), largest / len(split))
        return jnp.repeat(jnp.exp(steps), dims[dim] // parts).reshape((-1,) + (1,) * (len(dims) - dim - 1))

    loudness = one(*split[0])
    for cut in split[1:]:
        loudness = loudness * one(*cut)
    return loudness


def bell_draw(own_key, shape, spread, most, shards=(), held_as=jnp.bfloat16):
    values = spread * jax.random.normal(own_key, shape, jnp.float32)
    if shards:
        values = values * levels(own_key, shape, shards, -0.22, 0.18)
    return jnp.clip(values, -most, most).astype(held_as)


def setup_inputs(seed: int = 0) -> dict:
    keys = jax.random.split(jax.random.key(seed), 3)
    return {
        "orbitals": bell_draw(keys[0], (NX, NY, NZ, ORBS), 1.0, 6.0, ((0, 4), (3, 8)), jnp.float32),
        "potential": jnp.clip(2.0 * jax.random.uniform(keys[1], (NX, NY, NZ), jnp.float32) ** levels(keys[1], (NX, NY, NZ), ((0, 4),), -0.2, 0.2), 0.0, 2.0),
    }


STENCIL = (-205.0 / 72.0, 8.0 / 5.0, -1.0 / 5.0, 8.0 / 315.0, -1.0 / 560.0)
SHIFT_MID = 7.25
HALF_WIDTH = 4.75

def hamilton(field, potential):
    laplace = 3.0 * STENCIL[0] * field
    for axis in range(3):
        for offset in range(1, 5):
            laplace = laplace + STENCIL[offset] * (jnp.roll(field, offset, axis) + jnp.roll(field, -offset, axis))
    return -0.5 * laplace + potential[..., None] * field

def chebyshev(block, potential):
    before = block
    current = (hamilton(block, potential) - SHIFT_MID * block) / HALF_WIDTH
    for order in range(DEGREE - 1):
        following = 2.0 * (hamilton(current, potential) - SHIFT_MID * current) / HALF_WIDTH - before
        before, current = (current, following)
    return current

def reference(orbitals, potential):
    points = NX * NY * NZ
    trail = ORB_DEV - PANEL_DEV
    blocks = jnp.moveaxis(orbitals.reshape(NX, NY, NZ, N_ORB, ORB_DEV), 3, 0)
    filtered = lax.map(lambda block: chebyshev(block, potential), blocks)
    panel = jnp.moveaxis(filtered[..., :PANEL_DEV], 0, 3).reshape(points, PANEL)
    trailing = jnp.moveaxis(filtered[..., PANEL_DEV:], 0, 3).reshape(points, N_ORB * trail)
    highest = lax.Precision.HIGHEST
    gram_full = jnp.dot(panel.T, panel, precision=highest) / points
    coupling = jnp.dot(panel.T, trailing, precision=highest) / points
    lower_factor = jnp.linalg.cholesky(gram_full)
    identity = jnp.eye(PANEL, dtype=jnp.float32)
    inverse = lax.linalg.triangular_solve(lower_factor, identity, left_side=True, lower=True)
    ortho = jnp.dot(panel, inverse.T, precision=highest)
    middle = jnp.dot(inverse, coupling, precision=highest)
    project = jnp.dot(inverse.T, middle, precision=highest)
    trailing_new = trailing - jnp.dot(panel, project, precision=highest)
    joined = jnp.concatenate([ortho.reshape(points, N_ORB, PANEL_DEV), trailing_new.reshape(points, N_ORB, trail)], axis=2)
    return joined.reshape(NX, NY, NZ, N_ORB * ORB_DEV)
```

```python
import functools

import jax
import jax.numpy as jnp
from jax import lax
from jax.experimental import pallas as pl
from jax.experimental.pallas import tpu as pltpu
from jax.sharding import PartitionSpec as P

PANEL = 512
DEGREE = 4

STENCIL = (-205.0 / 72.0, 8.0 / 5.0, -1.0 / 5.0, 8.0 / 315.0, -1.0 / 560.0)
SHIFT_MID = 7.25
HALF_WIDTH = 4.75
LANES = 128
REACH = 4
MESH = pl.DeviceIdType.MESH
HIGHEST = lax.Precision.HIGHEST


def dot(a, b, dims):
    return lax.dot_general(
        a, b, ((dims[:1], dims[1:]), ((), ())), precision=HIGHEST, preferred_element_type=jnp.float32
    )


def regroup(load, store, count, rows):
    width = LANES // count
    step = min(rows, max(8, 128 // count))
    group = lax.broadcasted_iota(jnp.int32, (step, LANES), 1) // width

    def body(block, carry):
        here = pl.ds(pl.multiple_of(block * step, step), step)
        parts = [load(r, here) for r in range(count)]
        for j in range(count):
            out = None
            for r in range(count):
                turn = ((r - j) * width) % LANES
                piece = pltpu.roll(parts[r], turn, 1) if turn else parts[r]
                out = piece if out is None else jnp.where(group == r, piece, out)
            store(j, here, out)
        return carry

    lax.fori_loop(0, rows // step, body, 0)


def exchange(slots, here, send_sem, recv_sem, send, land):
    copies = []
    for hop in range(1, slots):
        there = lax.rem(here + hop, slots)
        copy = pltpu.make_async_remote_copy(
            src_ref=send(there),
            dst_ref=land.at[here],
            send_sem=send_sem.at[hop],
            recv_sem=recv_sem.at[hop],
            device_id={"space": there},
            device_id_type=MESH,
        )
        copy.start()
        copies.append(copy)
    return copies


def wait_exchange(slots, here, send_sem, recv_sem, send, land):
    for hop in range(1, slots):
        there = lax.rem(here + hop, slots)
        source = lax.rem(here + slots - hop, slots)
        pltpu.make_async_remote_copy(
            src_ref=send(there),
            dst_ref=land.at[source],
            send_sem=send_sem.at[hop],
            recv_sem=recv_sem.at[hop],
            device_id={"space": there},
            device_id_type=MESH,
        ).wait()


def gather_orb(count, me, buf, send_sem, recv_sem, side_send, side_recv):
    chips = count // 2
    chip, core = me // 2, lax.rem(me, 2)
    partner = chip * 2 + (1 - core)

    def along(origin, to, way, step):
        slot = buf.at[origin * 2 + core]
        return pltpu.make_async_remote_copy(
            src_ref=slot,
            dst_ref=slot,
            send_sem=send_sem.at[way, step],
            recv_sem=recv_sem.at[way, step],
            device_id={"orb": to * 2 + core},
            device_id_type=MESH,
        )

    def across(origin, side, index):
        slot = buf.at[origin * 2 + side]
        return pltpu.make_async_remote_copy(
            src_ref=slot,
            dst_ref=slot,
            send_sem=side_send.at[index],
            recv_sem=side_recv.at[index],
            device_id={"orb": partner},
            device_id_type=MESH,
        )

    steps = chips - 1
    for step in range(steps):
        @pl.when((chip - step >= 0) & (chip + 1 < chips))
        def _():
            along(chip - step, chip + 1, 0, step).start()

        @pl.when((chip + step < chips) & (chip - 1 >= 0))
        def _():
            along(chip + step, chip - 1, 1, step).start()

        if step == 0:
            across(chip, core, 0).start()

        @pl.when(chip - 1 - step >= 0)
        def _():
            along(chip - 1 - step, chip, 0, step).wait_recv()
            across(chip - 1 - step, core, 1 + step).start()

        @pl.when(chip + 1 + step < chips)
        def _():
            along(chip + 1 + step, chip, 1, step).wait_recv()
            across(chip + 1 + step, core, 1 + steps + step).start()

    across(chip, core, 0).wait_send()
    across(chip, 1 - core, 0).wait_recv()
    for step in range(steps):
        @pl.when((chip - step >= 0) & (chip + 1 < chips))
        def _():
            along(chip - step, chip + 1, 0, step).wait_send()

        @pl.when((chip + step < chips) & (chip - 1 >= 0))
        def _():
            along(chip + step, chip - 1, 1, step).wait_send()

        @pl.when(chip - 1 - step >= 0)
        def _():
            across(chip - 1 - step, core, 1 + step).wait_send()
            across(chip - 1 - step, 1 - core, 1 + step).wait_recv()

        @pl.when(chip + 1 + step < chips)
        def _():
            across(chip + 1 + step, core, 1 + steps + step).wait_send()
            across(chip + 1 + step, 1 - core, 1 + steps + step).wait_recv()


def filter_kernel(
    slabs, orbs, shape,
    x_ref, pot_ref, own_ref, panel_ref, gram_ref, cross_ref,
    pack, land, pack_back, land_back, pot_land, wide_a, wide_b, level, gath, part, part_land, rows_land,
    a_send, a_recv, p_send, p_recv, b_send, b_recv, c_send, c_recv,
    g_send, g_recv, gs_send, gs_recv, h_send, h_recv, hs_send, hs_recv,
):
    planes, rows_y, rows_z = shape
    points = planes * rows_y * rows_z
    here, me = lax.axis_index("space"), lax.axis_index("orb")
    chunk = points // slabs
    width = LANES // slabs

    barrier = pltpu.get_barrier_semaphore()
    for hop in range(1, slabs):
        pl.semaphore_signal(
            barrier, inc=1, device_id={"space": lax.rem(here + hop, slabs)}, device_id_type=MESH
        )
    for hop in range(1, orbs):
        pl.semaphore_signal(
            barrier, inc=1, device_id={"orb": lax.rem(me + hop, orbs)}, device_id_type=MESH
        )
    pl.semaphore_wait(barrier, slabs - 1 + orbs - 1)

    exchange(slabs, here, p_send, p_recv, lambda there: pot_ref, pot_land)

    def store_pack(j, at, value):
        pack[j, at, :] = value

    regroup(lambda r, at: x_ref[pl.ds(r * chunk + at.start, at.size), :], store_pack, slabs, chunk)
    exchange(slabs, here, a_send, a_recv, lambda there: pack.at[there], land)
    land[here] = pack[here]
    pot_land[here] = pot_ref[...]
    wait_exchange(slabs, here, p_send, p_recv, lambda there: pot_ref, pot_land)

    thin = points // LANES
    lane_group = lax.broadcasted_iota(jnp.int32, (thin, LANES), 1) // width
    fields = [pot_land[s] for s in range(slabs)]
    for l in range(LANES):
        value = None
        for s in range(slabs):
            spread = jnp.broadcast_to(fields[s][:, l : l + 1], (thin, LANES))
            value = spread if value is None else jnp.where(lane_group == s, spread, value)
        level[pl.ds(l * thin, thin), :] = (value - (SHIFT_MID + 1.5 * STENCIL[0])) * (1.0 / HALF_WIDTH)

    wait_exchange(slabs, here, a_send, a_recv, lambda there: pack.at[there], land)

    def put(target, row, value):
        target[pl.ds(points + row, value.shape[0]), :] = value
        target[pl.ds(row, value.shape[0]), :] = pltpu.roll(value, width, 1)
        target[pl.ds(2 * points + row, value.shape[0]), :] = pltpu.roll(value, LANES - width, 1)

    regroup(
        lambda r, at: land[r, at, :],
        lambda j, at, value: put(wide_a, j * chunk + at.start, value),
        slabs, chunk,
    )

    plane = rows_y * rows_z
    taps = [-0.5 * c / HALF_WIDTH for c in STENCIL]

    def sweep(source, target, first):
        def body(y, carry):
            for p in range(planes):
                def line(q, yy):
                    return source[pl.ds(pl.multiple_of(points + q * plane + yy * rows_z, rows_z), rows_z), :]

                row = pl.multiple_of(p * plane + y * rows_z, rows_z)
                centre = line(p, y)
                total = level[pl.ds(row, rows_z), :] * centre
                for m in range(1, REACH + 1):
                    near = line(p + m, y) + line(p - m, y)
                    near += line(p, lax.rem(y + m, rows_y)) + line(p, lax.rem(y + rows_y - m, rows_y))
                    near += pltpu.roll(centre, m, 0) + pltpu.roll(centre, rows_z - m, 0)
                    total += taps[m] * near
                if not first:
                    before = target[pl.ds(pl.multiple_of(points + row, rows_z), rows_z), :]
                    total = 2.0 * total - before
                put(target, row, total)
            return carry

        lax.fori_loop(0, rows_y, body, 0)

    sweep(wide_a, wide_b, True)
    source, target = wide_b, wide_a
    for _ in range(DEGREE - 1):
        sweep(source, target, False)
        source, target = target, source

    def store_back(j, at, value):
        pack_back[j, at, :] = value

    regroup(
        lambda r, at: source[pl.ds(points + r * chunk + at.start, at.size), :], store_back, slabs, chunk
    )
    exchange(slabs, here, b_send, b_recv, lambda there: pack_back.at[there], land_back)
    land_back[here] = pack_back[here]
    wait_exchange(slabs, here, b_send, b_recv, lambda there: pack_back.at[there], land_back)

    def store_own(j, at, value):
        own_ref[pl.ds(j * chunk + at.start, at.size), :] = value

    regroup(lambda r, at: land_back[r, at, :], store_own, slabs, chunk)

    panel_dev = PANEL // orbs
    folds = LANES // panel_dev
    fold = points // folds
    step = min(fold, 32)
    fold_group = lax.broadcasted_iota(jnp.int32, (step, LANES), 1) // panel_dev

    def folded(block, carry):
        at = pl.multiple_of(block * step, step)
        out = None
        for r in range(folds):
            piece = own_ref[pl.ds(r * fold + at, step), :]
            piece = pltpu.roll(piece, r * panel_dev, 1) if r else piece
            out = piece if out is None else jnp.where(fold_group == r, piece, out)
        gath[me, pl.ds(at, step), :] = out
        return carry

    lax.fori_loop(0, fold // step, folded, 0)
    gather_orb(orbs, me, gath, g_send, g_recv, gs_send, gs_recv)

    for tile in range(PANEL // LANES):
        def store_panel(j, at, value):
            panel_ref[pl.ds(j * fold + at.start, at.size), tile * LANES : (tile + 1) * LANES] = value

        regroup(lambda r, at: gath[tile * folds + r, at, :], store_panel, folds, fold)

    part[...] = jnp.zeros_like(part)
    block = 512

    def product(k, carry):
        at = pl.ds(pl.multiple_of(k * block, block), block)
        part[...] += dot(own_ref[at, :], panel_ref[at, :], (0, 0))
        return carry

    lax.fori_loop(0, points // block, product, 0)
    exchange(slabs, here, c_send, c_recv, lambda there: part, part_land)
    part_land[here] = part[...]
    wait_exchange(slabs, here, c_send, c_recv, lambda there: part, part_land)
    total = part_land[0]
    for s in range(1, slabs):
        total += part_land[s]
    total = total / (points * slabs)
    cross_ref[...] = total
    rows_land[me] = total[:panel_dev]
    gather_orb(orbs, me, rows_land, h_send, h_recv, hs_send, hs_recv)
    for o in range(orbs):
        gram_ref[o * panel_dev : (o + 1) * panel_dev, :] = rows_land[o]


def block_inverse(a):
    n = LANES
    tiles = n // 8
    rows = lax.broadcasted_iota(jnp.int32, (8, n), 0)
    cols = lax.broadcasted_iota(jnp.int32, (8, n), 1)
    work = [a[8 * t : 8 * t + 8] for t in range(tiles)]
    unit = [jnp.where(rows + 8 * t == cols, 1.0, 0.0).astype(jnp.float32) for t in range(tiles)]
    for j in range(n - 1):
        t0, s = divmod(j, 8)
        pivot = jnp.broadcast_to(work[t0][s : s + 1, j : j + 1], (1, n))
        scale = 1.0 / pivot
        row = jnp.broadcast_to(work[t0][s : s + 1] * scale, (8, n))
        other = jnp.broadcast_to(unit[t0][s : s + 1] * scale, (8, n))
        for t in range(t0, tiles):
            column = jnp.broadcast_to(work[t][:, j : j + 1], (8, n))
            if t == t0:
                column = jnp.where(rows > s, column, 0.0)
            work[t] = work[t] - column * row
            unit[t] = unit[t] - column * other
    out = []
    for t in range(tiles):
        pivots = jnp.sum(jnp.where(rows + 8 * t == cols, work[t], 0.0), axis=1, keepdims=True)
        out.append(unit[t] * (1.0 / jnp.sqrt(pivots)))
    return jnp.concatenate(out, axis=0)


def solve_kernel(orbs, own_ref, panel_ref, gram_ref, cross_ref, out_ref, work, inverse, weights):
    panel_dev = PANEL // orbs
    me = lax.axis_index("orb")
    n = LANES
    blocks = PANEL // n
    work[...] = gram_ref[...]
    inverse[...] = jnp.zeros_like(inverse)

    def factor(b, carry):
        at = pl.multiple_of(b * n, n)
        diag = block_inverse(work[pl.ds(at, n), pl.ds(at, n)])
        inverse[pl.ds(at, n), pl.ds(at, n)] = diag
        for i in range(1, blocks):
            @pl.when(i > b)
            def _():
                work[i * n : (i + 1) * n, pl.ds(at, n)] = dot(
                    work[i * n : (i + 1) * n, pl.ds(at, n)], diag, (1, 1)
                )
        for i in range(1, blocks):
            @pl.when(i > b)
            def _():
                left = work[i * n : (i + 1) * n, pl.ds(at, n)]
                for k in range(1, i + 1):
                    @pl.when(k > b)
                    def _():
                        right = work[k * n : (k + 1) * n, pl.ds(at, n)]
                        work[i * n : (i + 1) * n, k * n : (k + 1) * n] -= dot(left, right, (1, 1))
        return carry

    lax.fori_loop(0, blocks, factor, 0)
    for i in range(1, blocks):
        span = i * n
        inner = dot(work[i * n : (i + 1) * n, :span], inverse[:span, :span], (1, 0))
        inverse[i * n : (i + 1) * n, :span] = -dot(
            inverse[i * n : (i + 1) * n, i * n : (i + 1) * n], inner, (1, 0)
        )

    middle = dot(cross_ref[...], inverse[...], (1, 1))
    weights[...] = -dot(middle, inverse[...], (1, 0))
    weights[:panel_dev, :] = inverse[pl.ds(pl.multiple_of(me * panel_dev, panel_dev), panel_dev), :]
    points = own_ref.shape[0]
    block = 256
    lanes = lax.broadcasted_iota(jnp.int32, (block, LANES), 1)

    def final(k, carry):
        at = pl.ds(pl.multiple_of(k * block, block), block)
        kept = jnp.where(lanes < panel_dev, 0.0, own_ref[at, :])
        out_ref[at, :] = kept + dot(panel_ref[at, :], weights[...], (1, 1))
        return carry

    lax.fori_loop(0, points // block, final, 0)


def per_device(slabs, orbs, orbitals, potential):
    planes, rows_y, rows_z, columns = orbitals.shape
    points = planes * rows_y * rows_z
    panel_dev = PANEL // orbs
    folds = LANES // panel_dev
    thin = points // LANES
    f32 = jnp.float32
    vmem = pl.BlockSpec(memory_space=pltpu.VMEM)
    dma = pltpu.SemaphoreType.DMA
    steps = max(orbs // 2 - 1, 1)
    flat = orbitals.reshape(points, columns)
    own, panel, gram, cross = pl.pallas_call(
        functools.partial(filter_kernel, slabs, orbs, (planes, rows_y, rows_z)),
        out_shape=[
            jax.ShapeDtypeStruct((points, LANES), f32),
            jax.ShapeDtypeStruct((points, PANEL), f32),
            jax.ShapeDtypeStruct((PANEL, PANEL), f32),
            jax.ShapeDtypeStruct((LANES, PANEL), f32),
        ],
        in_specs=[vmem] * 2,
        out_specs=[vmem] * 4,
        scratch_shapes=[pltpu.VMEM((slabs, points // slabs, LANES), f32)] * 4
        + [
            pltpu.VMEM((slabs, thin, LANES), f32),
            pltpu.VMEM((3 * points, LANES), f32),
            pltpu.VMEM((3 * points, LANES), f32),
            pltpu.VMEM((points, LANES), f32),
            pltpu.VMEM((orbs, points // folds, LANES), f32),
            pltpu.VMEM((LANES, PANEL), f32),
            pltpu.VMEM((slabs, LANES, PANEL), f32),
            pltpu.VMEM((orbs, panel_dev, PANEL), f32),
        ]
        + [dma((slabs,))] * 8
        + [dma((2, steps))] * 2 + [dma((2 * steps + 1,))] * 2
        + [dma((2, steps))] * 2 + [dma((2 * steps + 1,))] * 2,
        compiler_params=pltpu.CompilerParams(
            collective_id=0, has_side_effects=True, vmem_limit_bytes=48 << 20
        ),
    )(flat, potential.reshape(LANES, thin).T)
    out = pl.pallas_call(
        functools.partial(solve_kernel, orbs),
        out_shape=jax.ShapeDtypeStruct((points, LANES), f32),
        in_specs=[vmem] * 4,
        out_specs=vmem,
        scratch_shapes=[
            pltpu.VMEM((PANEL, PANEL), f32),
            pltpu.VMEM((PANEL, PANEL), f32),
            pltpu.VMEM((LANES, PANEL), f32),
        ],
        compiler_params=pltpu.CompilerParams(vmem_limit_bytes=32 << 20),
    )(own, panel, gram, cross)
    return out.reshape(planes, rows_y, rows_z, columns)


def solution(mesh):
    placed = (P("space", None, None, "orb"), P("space", None, None))
    return jax.shard_map(
        functools.partial(per_device, mesh.shape["space"], mesh.shape["orb"]),
        mesh=mesh,
        in_specs=placed,
        out_specs=P("space", None, None, "orb"),
        check_vma=False,
    )
```

```python
import functools

import jax
import jax.numpy as jnp
from jax import lax
from jax.experimental import pallas as pl
from jax.experimental.pallas import tpu as pltpu
from jax.sharding import PartitionSpec as P

PANEL = 512
DEGREE = 4

STENCIL = (-205.0 / 72.0, 8.0 / 5.0, -1.0 / 5.0, 8.0 / 315.0, -1.0 / 560.0)
SHIFT_MID = 7.25
HALF_WIDTH = 4.75
LANES = 128
REACH = 4
MESH = pl.DeviceIdType.MESH
HIGHEST = lax.Precision.HIGHEST


def dot(a, b, dims):
    return lax.dot_general(
        a, b, ((dims[:1], dims[1:]), ((), ())), precision=HIGHEST, preferred_element_type=jnp.float32
    )


def regroup(load, store, count, rows):
    width = LANES // count
    step = min(rows, max(8, 128 // count))
    group = lax.broadcasted_iota(jnp.int32, (step, LANES), 1) // width

    def body(block, carry):
        here = pl.ds(pl.multiple_of(block * step, step), step)
        parts = [load(r, here) for r in range(count)]
        for j in range(count):
            out = None
            for r in range(count):
                turn = ((r - j) * width) % LANES
                piece = pltpu.roll(parts[r], turn, 1) if turn else parts[r]
                out = piece if out is None else jnp.where(group == r, piece, out)
            store(j, here, out)
        return carry

    lax.fori_loop(0, rows // step, body, 0)


def exchange(slots, here, send_sem, recv_sem, send, land):
    copies = []
    for hop in range(1, slots):
        there = lax.rem(here + hop, slots)
        copy = pltpu.make_async_remote_copy(
            src_ref=send(there),
            dst_ref=land.at[here],
            send_sem=send_sem.at[hop],
            recv_sem=recv_sem.at[hop],
            device_id={"space": there},
            device_id_type=MESH,
        )
        copy.start()
        copies.append(copy)
    return copies


def wait_exchange(slots, here, send_sem, recv_sem, send, land):
    for hop in range(1, slots):
        there = lax.rem(here + hop, slots)
        source = lax.rem(here + slots - hop, slots)
        pltpu.make_async_remote_copy(
            src_ref=send(there),
            dst_ref=land.at[source],
            send_sem=send_sem.at[hop],
            recv_sem=recv_sem.at[hop],
            device_id={"space": there},
            device_id_type=MESH,
        ).wait()


def gather_orb(count, me, buf, send_sem, recv_sem, side_send, side_recv, arrived=lambda chip: None):
    chips = count // 2
    chip, core = me // 2, lax.rem(me, 2)
    partner = chip * 2 + (1 - core)

    def along(origin, to, way, step):
        slot = buf.at[origin * 2 + core]
        return pltpu.make_async_remote_copy(
            src_ref=slot,
            dst_ref=slot,
            send_sem=send_sem.at[way, step],
            recv_sem=recv_sem.at[way, step],
            device_id={"orb": to * 2 + core},
            device_id_type=MESH,
        )

    def across(origin, side, index):
        slot = buf.at[origin * 2 + side]
        return pltpu.make_async_remote_copy(
            src_ref=slot,
            dst_ref=slot,
            send_sem=side_send.at[index],
            recv_sem=side_recv.at[index],
            device_id={"orb": partner},
            device_id_type=MESH,
        )

    steps = chips - 1

    def finish(step):
        @pl.when(chip - 1 - step >= 0)
        def _():
            across(chip - 1 - step, 1 - core, 1 + step).wait_recv()
            arrived(chip - 1 - step)

        @pl.when(chip + 1 + step < chips)
        def _():
            across(chip + 1 + step, 1 - core, 1 + steps + step).wait_recv()
            arrived(chip + 1 + step)

    for step in range(steps):
        @pl.when((chip - step >= 0) & (chip + 1 < chips))
        def _():
            along(chip - step, chip + 1, 0, step).start()

        @pl.when((chip + step < chips) & (chip - 1 >= 0))
        def _():
            along(chip + step, chip - 1, 1, step).start()

        if step == 0:
            across(chip, core, 0).start()
            across(chip, 1 - core, 0).wait_recv()
            arrived(chip)
        else:
            finish(step - 1)

        @pl.when(chip - 1 - step >= 0)
        def _():
            along(chip - 1 - step, chip, 0, step).wait_recv()
            across(chip - 1 - step, core, 1 + step).start()

        @pl.when(chip + 1 + step < chips)
        def _():
            along(chip + 1 + step, chip, 1, step).wait_recv()
            across(chip + 1 + step, core, 1 + steps + step).start()

    finish(steps - 1)
    across(chip, core, 0).wait_send()
    for step in range(steps):
        @pl.when((chip - step >= 0) & (chip + 1 < chips))
        def _():
            along(chip - step, chip + 1, 0, step).wait_send()

        @pl.when((chip + step < chips) & (chip - 1 >= 0))
        def _():
            along(chip + step, chip - 1, 1, step).wait_send()

        @pl.when(chip - 1 - step >= 0)
        def _():
            across(chip - 1 - step, core, 1 + step).wait_send()

        @pl.when(chip + 1 + step < chips)
        def _():
            across(chip + 1 + step, core, 1 + steps + step).wait_send()


def filter_kernel(
    slabs, orbs, shape,
    x_ref, pot_ref, own_ref, panel_ref, gram_ref, cross_ref,
    pack, land, pack_back, land_back, pot_land, wide_a, wide_b, level, gath, part, part_land, rows_land,
    a_send, a_recv, p_send, p_recv, b_send, b_recv, c_send, c_recv, d_send, d_recv,
    g_send, g_recv, gs_send, gs_recv, h_send, h_recv, hs_send, hs_recv,
):
    planes, rows_y, rows_z = shape
    points = planes * rows_y * rows_z
    here, me = lax.axis_index("space"), lax.axis_index("orb")
    chunk = points // slabs
    width = LANES // slabs

    barrier = pltpu.get_barrier_semaphore()
    for hop in range(1, slabs):
        pl.semaphore_signal(
            barrier, inc=1, device_id={"space": lax.rem(here + hop, slabs)}, device_id_type=MESH
        )
    for hop in range(1, orbs):
        pl.semaphore_signal(
            barrier, inc=1, device_id={"orb": lax.rem(me + hop, orbs)}, device_id_type=MESH
        )
    pl.semaphore_wait(barrier, slabs - 1 + orbs - 1)

    exchange(slabs, here, p_send, p_recv, lambda there: pot_ref, pot_land)

    def store_pack(j, at, value):
        pack[j, at, :] = value

    regroup(lambda r, at: x_ref[pl.ds(r * chunk + at.start, at.size), :], store_pack, slabs, chunk)
    exchange(slabs, here, a_send, a_recv, lambda there: pack.at[there], land)
    land[here] = pack[here]
    pot_land[here] = pot_ref[...]
    wait_exchange(slabs, here, p_send, p_recv, lambda there: pot_ref, pot_land)

    thin = points // LANES
    lane_group = lax.broadcasted_iota(jnp.int32, (thin, LANES), 1) // width
    fields = [pot_land[s] for s in range(slabs)]
    for l in range(LANES):
        value = None
        for s in range(slabs):
            spread = jnp.broadcast_to(fields[s][:, l : l + 1], (thin, LANES))
            value = spread if value is None else jnp.where(lane_group == s, spread, value)
        level[pl.ds(l * thin, thin), :] = (value - (SHIFT_MID + 1.5 * STENCIL[0])) * (1.0 / HALF_WIDTH)

    wait_exchange(slabs, here, a_send, a_recv, lambda there: pack.at[there], land)

    def put(target, row, value):
        target[pl.ds(points + row, value.shape[0]), :] = value
        target[pl.ds(row, value.shape[0]), :] = pltpu.roll(value, width, 1)
        target[pl.ds(2 * points + row, value.shape[0]), :] = pltpu.roll(value, LANES - width, 1)

    regroup(
        lambda r, at: land[r, at, :],
        lambda j, at, value: put(wide_a, j * chunk + at.start, value),
        slabs, chunk,
    )

    plane = rows_y * rows_z
    taps = [-0.5 * c / HALF_WIDTH for c in STENCIL]

    def sweep(source, target, first):
        def body(y, carry):
            for p in range(planes):
                def line(q, yy):
                    return source[pl.ds(pl.multiple_of(points + q * plane + yy * rows_z, rows_z), rows_z), :]

                row = pl.multiple_of(p * plane + y * rows_z, rows_z)
                centre = line(p, y)
                total = level[pl.ds(row, rows_z), :] * centre
                for m in range(1, REACH + 1):
                    near = line(p + m, y) + line(p - m, y)
                    near += line(p, lax.rem(y + m, rows_y)) + line(p, lax.rem(y + rows_y - m, rows_y))
                    near += pltpu.roll(centre, m, 0) + pltpu.roll(centre, rows_z - m, 0)
                    total += taps[m] * near
                if not first:
                    before = target[pl.ds(pl.multiple_of(points + row, rows_z), rows_z), :]
                    total = 2.0 * total - before
                put(target, row, total)
            return carry

        lax.fori_loop(0, rows_y, body, 0)

    sweep(wide_a, wide_b, True)
    source, target = wide_b, wide_a
    for _ in range(DEGREE - 1):
        sweep(source, target, False)
        source, target = target, source

    def store_back(j, at, value):
        pack_back[j, at, :] = value

    regroup(
        lambda r, at: source[pl.ds(points + r * chunk + at.start, at.size), :], store_back, slabs, chunk
    )
    exchange(slabs, here, b_send, b_recv, lambda there: pack_back.at[there], land_back)
    land_back[here] = pack_back[here]
    wait_exchange(slabs, here, b_send, b_recv, lambda there: pack_back.at[there], land_back)

    def store_own(j, at, value):
        own_ref[pl.ds(j * chunk + at.start, at.size), :] = value

    regroup(lambda r, at: land_back[r, at, :], store_own, slabs, chunk)

    panel_dev = PANEL // orbs
    folds = LANES // panel_dev
    fold = points // folds
    step = min(fold, 32)
    fold_group = lax.broadcasted_iota(jnp.int32, (step, LANES), 1) // panel_dev

    def folded(block, carry):
        at = pl.multiple_of(block * step, step)
        out = None
        for r in range(folds):
            piece = own_ref[pl.ds(r * fold + at, step), :]
            piece = pltpu.roll(piece, r * panel_dev, 1) if r else piece
            out = piece if out is None else jnp.where(fold_group == r, piece, out)
        gath[me, pl.ds(at, step), :] = out
        return carry

    lax.fori_loop(0, fold // step, folded, 0)

    block = 512

    def take(tile):
        lanes = pl.ds(pl.multiple_of(tile * LANES, LANES), LANES)

        def store_panel(j, at, value):
            panel_ref[pl.ds(j * fold + at.start, at.size), lanes] = value

        regroup(lambda r, at: gath[tile * folds + r, at, :], store_panel, folds, fold)

        def product(k, total):
            at = pl.ds(pl.multiple_of(k * block, block), block)
            return total + dot(own_ref[at, :], panel_ref[at, lanes], (0, 0))

        part[:, lanes] = lax.fori_loop(
            0, points // block, product, jnp.zeros((LANES, LANES), jnp.float32)
        )

    if folds == 2:
        gather_orb(orbs, me, gath, g_send, g_recv, gs_send, gs_recv, take)
    else:
        gather_orb(orbs, me, gath, g_send, g_recv, gs_send, gs_recv)

        def each(tile, carry):
            take(tile)
            return carry

        lax.fori_loop(0, PANEL // LANES, each, 0)

    top, rest = part.at[:panel_dev], part.at[panel_dev:]
    top_land, rest_land = part_land.at[:, :panel_dev], part_land.at[:, panel_dev:]
    exchange(slabs, here, c_send, c_recv, lambda there: top, top_land)
    exchange(slabs, here, d_send, d_recv, lambda there: rest, rest_land)
    part_land[here] = part[...]
    points_all = points * slabs

    def summed(view):
        total = view[0]
        for s in range(1, slabs):
            total += view[s]
        return total / points_all

    wait_exchange(slabs, here, c_send, c_recv, lambda there: top, top_land)
    rows_land[me] = summed(top_land)
    gather_orb(orbs, me, rows_land, h_send, h_recv, hs_send, hs_recv)
    wait_exchange(slabs, here, d_send, d_recv, lambda there: rest, rest_land)
    cross_ref[:panel_dev, :] = jnp.zeros((panel_dev, PANEL), jnp.float32)
    cross_ref[panel_dev:, :] = summed(rest_land)
    for o in range(orbs):
        gram_ref[o * panel_dev : (o + 1) * panel_dev, :] = rows_land[o]


def block_inverse(a):
    n = LANES
    tiles = n // 8
    rows = lax.broadcasted_iota(jnp.int32, (8, n), 0)
    cols = lax.broadcasted_iota(jnp.int32, (8, n), 1)
    work = [a[8 * t : 8 * t + 8] for t in range(tiles)]
    unit = [jnp.where(rows + 8 * t == cols, 1.0, 0.0).astype(jnp.float32) for t in range(tiles)]
    for t0 in range(tiles):
        base = 8 * t0
        columns = [jnp.broadcast_to(work[t0][:, base + k : base + k + 1], (8, n)) for k in range(8)]
        small = {
            (i, k): jnp.broadcast_to(columns[k][i : i + 1], (8, n)) for i in range(8) for k in range(i + 1)
        }
        lower, scales = {}, []
        for j in range(8):
            scales.append(1.0 / small[j, j])
            for i in range(j + 1, 8):
                lower[i, j] = small[i, j] * scales[j]
            for i in range(j + 1, 8):
                for k in range(j + 1, i + 1):
                    small[i, k] = small[i, k] - lower[i, j] * small[k, j]
        turned = {}
        for j in range(8):
            for i in range(j + 1, 8):
                value = lower[i, j]
                for k in range(j + 1, i):
                    value = value + lower[i, k] * turned[k, j]
                turned[i, j] = -value
        a_row, u_row = work[t0], unit[t0]
        a_new, u_new = a_row, u_row
        for k in range(7):
            weight = jnp.zeros((8, n), jnp.float32)
            for i in range(k + 1, 8):
                weight = jnp.where(rows == i, turned[i, k], weight)
            a_new = a_new + weight * jnp.broadcast_to(a_row[k : k + 1], (8, n))
            u_new = u_new + weight * jnp.broadcast_to(u_row[k : k + 1], (8, n))
        work[t0], unit[t0] = a_new, u_new
        if t0 == tiles - 1:
            break
        a_out = u_out = None
        for i in range(8):
            weight = jnp.where(rows == i, scales[i], 0.0)
            for k in range(i):
                weight = jnp.where(rows == k, turned[i, k] * scales[i], weight)
            a_term = weight * jnp.broadcast_to(a_new[i : i + 1], (8, n))
            u_term = weight * jnp.broadcast_to(u_new[i : i + 1], (8, n))
            a_out = a_term if a_out is None else a_out + a_term
            u_out = u_term if u_out is None else u_out + u_term
        a_rows = [jnp.broadcast_to(a_out[k : k + 1], (8, n)) for k in range(8)]
        u_rows = [jnp.broadcast_to(u_out[k : k + 1], (8, n)) for k in range(8)]
        for t in range(t0 + 1, tiles):
            before = work[t]
            for k in range(8):
                column = jnp.broadcast_to(before[:, base + k : base + k + 1], (8, n))
                work[t] = work[t] - column * a_rows[k]
                unit[t] = unit[t] - column * u_rows[k]
    out = []
    for t in range(tiles):
        pivots = jnp.sum(jnp.where(rows + 8 * t == cols, work[t], 0.0), axis=1, keepdims=True)
        out.append(unit[t] * (1.0 / jnp.sqrt(pivots)))
    return jnp.concatenate(out, axis=0)


def solve_kernel(orbs, own_ref, panel_ref, gram_ref, cross_ref, out_ref, work, inverse, weights):
    panel_dev = PANEL // orbs
    me = lax.axis_index("orb")
    n = LANES
    blocks = PANEL // n
    work[...] = gram_ref[...]
    inverse[...] = jnp.zeros_like(inverse)

    def factor(b, carry):
        at = pl.multiple_of(b * n, n)
        diag = block_inverse(work[pl.ds(at, n), pl.ds(at, n)])
        inverse[pl.ds(at, n), pl.ds(at, n)] = diag
        for i in range(1, blocks):
            @pl.when(i > b)
            def _():
                work[i * n : (i + 1) * n, pl.ds(at, n)] = dot(
                    work[i * n : (i + 1) * n, pl.ds(at, n)], diag, (1, 1)
                )
        for i in range(1, blocks):
            @pl.when(i > b)
            def _():
                left = work[i * n : (i + 1) * n, pl.ds(at, n)]
                for k in range(1, i + 1):
                    @pl.when(k > b)
                    def _():
                        right = work[k * n : (k + 1) * n, pl.ds(at, n)]
                        work[i * n : (i + 1) * n, k * n : (k + 1) * n] -= dot(left, right, (1, 1))
        return carry

    lax.fori_loop(0, blocks, factor, 0)
    for i in range(1, blocks):
        span = i * n
        inner = dot(work[i * n : (i + 1) * n, :span], inverse[:span, :span], (1, 0))
        inverse[i * n : (i + 1) * n, :span] = -dot(
            inverse[i * n : (i + 1) * n, i * n : (i + 1) * n], inner, (1, 0)
        )

    middle = dot(cross_ref[...], inverse[...], (1, 1))
    weights[...] = -dot(middle, inverse[...], (1, 0))
    weights[:panel_dev, :] = inverse[pl.ds(pl.multiple_of(me * panel_dev, panel_dev), panel_dev), :]
    points = own_ref.shape[0]
    block = 256
    lanes = lax.broadcasted_iota(jnp.int32, (block, LANES), 1)

    def final(k, carry):
        at = pl.ds(pl.multiple_of(k * block, block), block)
        kept = jnp.where(lanes < panel_dev, 0.0, own_ref[at, :])
        out_ref[at, :] = kept + dot(panel_ref[at, :], weights[...], (1, 1))
        return carry

    lax.fori_loop(0, points // block, final, 0)


def per_device(slabs, orbs, orbitals, potential):
    planes, rows_y, rows_z, columns = orbitals.shape
    points = planes * rows_y * rows_z
    panel_dev = PANEL // orbs
    folds = LANES // panel_dev
    thin = points // LANES
    f32 = jnp.float32
    vmem = pl.BlockSpec(memory_space=pltpu.VMEM)
    dma = pltpu.SemaphoreType.DMA
    steps = max(orbs // 2 - 1, 1)
    flat = orbitals.reshape(points, columns)
    own, panel, gram, cross = pl.pallas_call(
        functools.partial(filter_kernel, slabs, orbs, (planes, rows_y, rows_z)),
        out_shape=[
            jax.ShapeDtypeStruct((points, LANES), f32),
            jax.ShapeDtypeStruct((points, PANEL), f32),
            jax.ShapeDtypeStruct((PANEL, PANEL), f32),
            jax.ShapeDtypeStruct((LANES, PANEL), f32),
        ],
        in_specs=[vmem] * 2,
        out_specs=[vmem] * 4,
        scratch_shapes=[pltpu.VMEM((slabs, points // slabs, LANES), f32)] * 4
        + [
            pltpu.VMEM((slabs, thin, LANES), f32),
            pltpu.VMEM((3 * points, LANES), f32),
            pltpu.VMEM((3 * points, LANES), f32),
            pltpu.VMEM((points, LANES), f32),
            pltpu.VMEM((orbs, points // folds, LANES), f32),
            pltpu.VMEM((LANES, PANEL), f32),
            pltpu.VMEM((slabs, LANES, PANEL), f32),
            pltpu.VMEM((orbs, panel_dev, PANEL), f32),
        ]
        + [dma((slabs,))] * 10
        + [dma((2, steps))] * 2 + [dma((2 * steps + 1,))] * 2
        + [dma((2, steps))] * 2 + [dma((2 * steps + 1,))] * 2,
        compiler_params=pltpu.CompilerParams(
            collective_id=0, has_side_effects=True, vmem_limit_bytes=48 << 20
        ),
    )(flat, potential.reshape(LANES, thin).T)
    out = pl.pallas_call(
        functools.partial(solve_kernel, orbs),
        out_shape=jax.ShapeDtypeStruct((points, LANES), f32),
        in_specs=[vmem] * 4,
        out_specs=vmem,
        scratch_shapes=[
            pltpu.VMEM((PANEL, PANEL), f32),
            pltpu.VMEM((PANEL, PANEL), f32),
            pltpu.VMEM((LANES, PANEL), f32),
        ],
        compiler_params=pltpu.CompilerParams(vmem_limit_bytes=32 << 20),
    )(own, panel, gram, cross)
    return out.reshape(planes, rows_y, rows_z, columns)


def solution(mesh):
    placed = (P("space", None, None, "orb"), P("space", None, None))
    return jax.shard_map(
        functools.partial(per_device, mesh.shape["space"], mesh.shape["orb"]),
        mesh=mesh,
        in_specs=placed,
        out_specs=P("space", None, None, "orb"),
        check_vma=False,
    )
```

```python
import functools

import jax
import jax.numpy as jnp
from jax import lax
from jax.experimental import pallas as pl
from jax.experimental.pallas import tpu as pltpu
from jax.sharding import PartitionSpec as P

PANEL = 512
DEGREE = 4

STENCIL = (-205.0 / 72.0, 8.0 / 5.0, -1.0 / 5.0, 8.0 / 315.0, -1.0 / 560.0)
SHIFT_MID = 7.25
HALF_WIDTH = 4.75
LANES = 128
REACH = 4
MESH = pl.DeviceIdType.MESH
HIGHEST = lax.Precision.HIGHEST


def dot(a, b, dims):
    return lax.dot_general(
        a, b, ((dims[:1], dims[1:]), ((), ())), precision=HIGHEST, preferred_element_type=jnp.float32
    )


def regroup(load, store, count, rows):
    width = LANES // count
    step = min(rows, max(8, 128 // count))
    group = lax.broadcasted_iota(jnp.int32, (step, LANES), 1) // width

    def body(block, carry):
        here = pl.ds(pl.multiple_of(block * step, step), step)
        parts = [load(r, here) for r in range(count)]
        for j in range(count):
            out = None
            for r in range(count):
                turn = ((r - j) * width) % LANES
                piece = pltpu.roll(parts[r], turn, 1) if turn else parts[r]
                out = piece if out is None else jnp.where(group == r, piece, out)
            store(j, here, out)
        return carry

    lax.fori_loop(0, rows // step, body, 0)


def exchange(slots, here, send_sem, recv_sem, send, land):
    copies = []
    for hop in range(1, slots):
        there = lax.rem(here + hop, slots)
        copy = pltpu.make_async_remote_copy(
            src_ref=send(there),
            dst_ref=land.at[here],
            send_sem=send_sem.at[hop],
            recv_sem=recv_sem.at[hop],
            device_id={"space": there},
            device_id_type=MESH,
        )
        copy.start()
        copies.append(copy)
    return copies


def wait_exchange(slots, here, send_sem, recv_sem, send, land):
    for hop in range(1, slots):
        there = lax.rem(here + hop, slots)
        source = lax.rem(here + slots - hop, slots)
        pltpu.make_async_remote_copy(
            src_ref=send(there),
            dst_ref=land.at[source],
            send_sem=send_sem.at[hop],
            recv_sem=recv_sem.at[hop],
            device_id={"space": there},
            device_id_type=MESH,
        ).wait()


def gather_orb(count, me, buf, send_sem, recv_sem, side_send, side_recv, arrived=lambda chip: None, during=None):
    chips = count // 2
    chip, core = me // 2, lax.rem(me, 2)
    partner = chip * 2 + (1 - core)

    def along(origin, to, way, step):
        slot = buf.at[origin * 2 + core]
        return pltpu.make_async_remote_copy(
            src_ref=slot,
            dst_ref=slot,
            send_sem=send_sem.at[way, step],
            recv_sem=recv_sem.at[way, step],
            device_id={"orb": to * 2 + core},
            device_id_type=MESH,
        )

    def across(origin, side, index):
        slot = buf.at[origin * 2 + side]
        return pltpu.make_async_remote_copy(
            src_ref=slot,
            dst_ref=slot,
            send_sem=side_send.at[index],
            recv_sem=side_recv.at[index],
            device_id={"orb": partner},
            device_id_type=MESH,
        )

    steps = chips - 1

    def finish(step):
        @pl.when(chip - 1 - step >= 0)
        def _():
            across(chip - 1 - step, 1 - core, 1 + step).wait_recv()
            arrived(chip - 1 - step)

        @pl.when(chip + 1 + step < chips)
        def _():
            across(chip + 1 + step, 1 - core, 1 + steps + step).wait_recv()
            arrived(chip + 1 + step)

    for step in range(steps):
        @pl.when((chip - step >= 0) & (chip + 1 < chips))
        def _():
            along(chip - step, chip + 1, 0, step).start()

        @pl.when((chip + step < chips) & (chip - 1 >= 0))
        def _():
            along(chip + step, chip - 1, 1, step).start()

        if step == 0:
            across(chip, core, 0).start()
            if during:
                during[0]()
        if step == (1 if during else 0):
            if during:
                during[1]()
            across(chip, 1 - core, 0).wait_recv()
            arrived(chip)
        if step:
            finish(step - 1)

        @pl.when(chip - 1 - step >= 0)
        def _():
            along(chip - 1 - step, chip, 0, step).wait_recv()
            across(chip - 1 - step, core, 1 + step).start()

        @pl.when(chip + 1 + step < chips)
        def _():
            along(chip + 1 + step, chip, 1, step).wait_recv()
            across(chip + 1 + step, core, 1 + steps + step).start()

    finish(steps - 1)
    across(chip, core, 0).wait_send()
    for step in range(steps):
        @pl.when((chip - step >= 0) & (chip + 1 < chips))
        def _():
            along(chip - step, chip + 1, 0, step).wait_send()

        @pl.when((chip + step < chips) & (chip - 1 >= 0))
        def _():
            along(chip + step, chip - 1, 1, step).wait_send()

        @pl.when(chip - 1 - step >= 0)
        def _():
            across(chip - 1 - step, core, 1 + step).wait_send()

        @pl.when(chip + 1 + step < chips)
        def _():
            across(chip + 1 + step, core, 1 + steps + step).wait_send()


def split_filter(
    slabs, shape, here, me, x_ref, pot_ref, own_ref, pack, land, pack_back, land_back, pot_land,
    wide_a, wide_b, level, gath, out_sems, pot_sems, back_sems,
):
    planes, rows_y, rows_z = shape
    points = planes * rows_y * rows_z
    slots = 2 * slabs
    width = LANES // slots
    rows = points // slots
    plane = 3 * rows
    thin = points // LANES
    step = 16
    slot = lax.broadcasted_iota(jnp.int32, (step, LANES), 1) // width

    def merge(parts):
        out = None
        for u, (value, v) in enumerate(parts):
            turn = ((u - v) * width) % LANES
            value = pltpu.roll(value, turn, 1) if turn else value
            out = value if out is None else jnp.where(slot == u, value, out)
        return out

    def over(body):
        def one(block, carry):
            body(pl.multiple_of(block * step, step))
            return carry

        lax.fori_loop(0, rows // step, one, 0)

    def half(buf, h):
        return buf.at[:, h * rows : (h + 1) * rows]

    def send(buf, landing, h, sems):
        exchange(slabs, here, *sems[h], lambda there: half(buf, h).at[there], half(landing, h))
        landing[here, h * rows : (h + 1) * rows] = buf[here, h * rows : (h + 1) * rows]

    def wait(buf, landing, h, sems):
        wait_exchange(slabs, here, *sems[h], lambda there: half(buf, h).at[there], half(landing, h))

    def pack_half(h):
        def body(at):
            parts = [x_ref[pl.ds(q * rows + at, step), :] for q in range(slots)]
            for j in range(slabs):
                pack[j, pl.ds(h * rows + at, step), :] = merge([(part, h * slabs + j) for part in parts])

        over(body)
        send(pack, land, h, out_sems)

    def put(target, p, row, value):
        odd = lax.rem(lax.broadcasted_iota(jnp.int32, value.shape, 1) // width, 2)
        size = value.shape[0]
        swapped = jnp.where(odd == 0, pltpu.roll(value, LANES - width, 1), pltpu.roll(value, width, 1))
        target[pl.ds((planes + p) * plane + rows + row, size), :] = value
        target[pl.ds((planes + p) * plane + row, size), :] = swapped
        target[pl.ds((planes + p) * plane + 2 * rows + row, size), :] = swapped
        target[pl.ds(p * plane + rows + row, size), :] = pltpu.roll(value, 2 * width, 1)
        target[pl.ds((2 * planes + p) * plane + rows + row, size), :] = pltpu.roll(value, LANES - 2 * width, 1)

    taps = [-0.5 * c / HALF_WIDTH for c in STENCIL]

    def sweep(source, target, first):
        def body(y, carry):
            for p in range(planes):
                def line(q, yy):
                    row = pl.multiple_of((planes + q) * plane + rows + yy * rows_z, rows_z)
                    return source[pl.ds(row, rows_z), :]

                row = pl.multiple_of(y * rows_z, rows_z)
                centre = line(p, y)
                total = level[pl.ds(p * rows + row, rows_z), :] * centre
                for m in range(1, REACH + 1):
                    near = line(p + m, y) + line(p - m, y) + line(p, y + m) + line(p, y - m)
                    near += pltpu.roll(centre, m, 0) + pltpu.roll(centre, rows_z - m, 0)
                    total += taps[m] * near
                if not first:
                    total = 2.0 * total - target[pl.ds((planes + p) * plane + rows + row, rows_z), :]
                put(target, p, row, total)
            return carry

        lax.fori_loop(0, rows_y // 2, body, 0)

    def filter_half(h):
        wait(pack, land, h, out_sems)

        def unpack(at):
            parts = [land[i, pl.ds(h * rows + at, step), :] for i in range(slabs)]
            for p in range(planes):
                put(wide_a, p, at, merge([(parts[u // 2], 2 * p + u % 2) for u in range(slots)]))

        over(unpack)
        sweep(wide_a, wide_b, True)
        source, target = wide_b, wide_a
        for _ in range(DEGREE - 1):
            sweep(source, target, False)
            source, target = target, source

        def body(at):
            parts = [source[pl.ds((planes + p) * plane + rows + at, step), :] for p in range(planes)]
            for i in range(slabs):
                pack_back[i, pl.ds(h * rows + at, step), :] = merge(
                    [(parts[q // 2], 2 * i + q % 2) for q in range(slots)]
                )

        over(body)
        send(pack_back, land_back, h, back_sems)

    pack_half(0)
    pack_half(1)
    pot_land[here] = pot_ref[...]
    wait_exchange(slabs, here, *pot_sems, lambda there: pot_ref, pot_land)
    lane_slot = lax.broadcasted_iota(jnp.int32, (thin, LANES), 1) // width
    fields = [pot_land[s] for s in range(slabs)]
    pieces = rows // thin
    for p in range(planes):
        for e in range(pieces):
            value = None
            for u in range(slots):
                l = (2 * p + u % 2) * pieces + e
                spread = jnp.broadcast_to(fields[u // 2][:, l : l + 1], (thin, LANES))
                value = spread if value is None else jnp.where(lane_slot == u, spread, value)
            level[pl.ds(p * rows + e * thin, thin), :] = (
                value - (SHIFT_MID + 1.5 * STENCIL[0])
            ) * (1.0 / HALF_WIDTH)

    filter_half(0)
    wait(pack_back, land_back, 0, back_sems)

    def fold_own(at):
        parts = [land_back[j, pl.ds(at, step), :] for j in range(slabs)]
        for k in range(slabs):
            gath[me, pl.ds(k * rows + at, step), :] = merge(
                [(parts[u % slabs], (u // slabs) * slabs + k) for u in range(slots)]
            )

    over(fold_own)

    def finish():
        wait(pack_back, land_back, 1, back_sems)

        def body(at):
            parts = [
                land_back[u % slabs, pl.ds((u // slabs) * rows + at, step), :] for u in range(slots)
            ]
            for q in range(slots):
                own_ref[pl.ds(q * rows + at, step), :] = merge([(part, q) for part in parts])

        over(body)

    return (lambda: filter_half(1)), finish


def filter_kernel(
    slabs, orbs, shape, split,
    x_ref, pot_ref, own_ref, panel_ref, gram_ref, cross_ref,
    pack, land, pack_back, land_back, pot_land, wide_a, wide_b, level, gath, part, part_land, rows_land,
    a_send, a_recv, p_send, p_recv, b_send, b_recv, c_send, c_recv, d_send, d_recv, e_send, e_recv, f_send, f_recv,
    g_send, g_recv, gs_send, gs_recv, h_send, h_recv, hs_send, hs_recv,
):
    planes, rows_y, rows_z = shape
    points = planes * rows_y * rows_z
    here, me = lax.axis_index("space"), lax.axis_index("orb")
    chunk = points // slabs
    width = LANES // slabs

    barrier = pltpu.get_barrier_semaphore()
    for hop in range(1, slabs):
        pl.semaphore_signal(
            barrier, inc=1, device_id={"space": lax.rem(here + hop, slabs)}, device_id_type=MESH
        )
    for hop in range(1, orbs):
        pl.semaphore_signal(
            barrier, inc=1, device_id={"orb": lax.rem(me + hop, orbs)}, device_id_type=MESH
        )
    pl.semaphore_wait(barrier, slabs - 1 + orbs - 1)

    exchange(slabs, here, p_send, p_recv, lambda there: pot_ref, pot_land)

    panel_dev = PANEL // orbs
    folds = LANES // panel_dev
    fold = points // folds
    during = None
    if split:
        during = split_filter(
            slabs, shape, here, me, x_ref, pot_ref, own_ref, pack, land, pack_back, land_back, pot_land,
            wide_a, wide_b, level, gath,
            ((a_send, a_recv), (e_send, e_recv)), (p_send, p_recv), ((b_send, b_recv), (f_send, f_recv)),
        )
    else:
        def store_pack(j, at, value):
            pack[j, at, :] = value

        regroup(lambda r, at: x_ref[pl.ds(r * chunk + at.start, at.size), :], store_pack, slabs, chunk)
        exchange(slabs, here, a_send, a_recv, lambda there: pack.at[there], land)
        land[here] = pack[here]
        pot_land[here] = pot_ref[...]
        wait_exchange(slabs, here, p_send, p_recv, lambda there: pot_ref, pot_land)

        thin = points // LANES
        lane_group = lax.broadcasted_iota(jnp.int32, (thin, LANES), 1) // width
        fields = [pot_land[s] for s in range(slabs)]
        for l in range(LANES):
            value = None
            for s in range(slabs):
                spread = jnp.broadcast_to(fields[s][:, l : l + 1], (thin, LANES))
                value = spread if value is None else jnp.where(lane_group == s, spread, value)
            level[pl.ds(l * thin, thin), :] = (value - (SHIFT_MID + 1.5 * STENCIL[0])) * (1.0 / HALF_WIDTH)

        wait_exchange(slabs, here, a_send, a_recv, lambda there: pack.at[there], land)

        def put(target, row, value):
            target[pl.ds(points + row, value.shape[0]), :] = value
            target[pl.ds(row, value.shape[0]), :] = pltpu.roll(value, width, 1)
            target[pl.ds(2 * points + row, value.shape[0]), :] = pltpu.roll(value, LANES - width, 1)

        regroup(
            lambda r, at: land[r, at, :],
            lambda j, at, value: put(wide_a, j * chunk + at.start, value),
            slabs, chunk,
        )

        plane = rows_y * rows_z
        taps = [-0.5 * c / HALF_WIDTH for c in STENCIL]

        def sweep(source, target, first):
            def body(y, carry):
                for p in range(planes):
                    def line(q, yy):
                        return source[pl.ds(pl.multiple_of(points + q * plane + yy * rows_z, rows_z), rows_z), :]

                    row = pl.multiple_of(p * plane + y * rows_z, rows_z)
                    centre = line(p, y)
                    total = level[pl.ds(row, rows_z), :] * centre
                    for m in range(1, REACH + 1):
                        near = line(p + m, y) + line(p - m, y)
                        near += line(p, lax.rem(y + m, rows_y)) + line(p, lax.rem(y + rows_y - m, rows_y))
                        near += pltpu.roll(centre, m, 0) + pltpu.roll(centre, rows_z - m, 0)
                        total += taps[m] * near
                    if not first:
                        before = target[pl.ds(pl.multiple_of(points + row, rows_z), rows_z), :]
                        total = 2.0 * total - before
                    put(target, row, total)
                return carry

            lax.fori_loop(0, rows_y, body, 0)

        sweep(wide_a, wide_b, True)
        source, target = wide_b, wide_a
        for _ in range(DEGREE - 1):
            sweep(source, target, False)
            source, target = target, source

        def store_back(j, at, value):
            pack_back[j, at, :] = value

        regroup(
            lambda r, at: source[pl.ds(points + r * chunk + at.start, at.size), :], store_back, slabs, chunk
        )
        exchange(slabs, here, b_send, b_recv, lambda there: pack_back.at[there], land_back)
        land_back[here] = pack_back[here]
        wait_exchange(slabs, here, b_send, b_recv, lambda there: pack_back.at[there], land_back)

        def store_own(j, at, value):
            own_ref[pl.ds(j * chunk + at.start, at.size), :] = value

        regroup(lambda r, at: land_back[r, at, :], store_own, slabs, chunk)

        step = min(fold, 32)
        fold_group = lax.broadcasted_iota(jnp.int32, (step, LANES), 1) // panel_dev

        def folded(block, carry):
            at = pl.multiple_of(block * step, step)
            out = None
            for r in range(folds):
                piece = own_ref[pl.ds(r * fold + at, step), :]
                piece = pltpu.roll(piece, r * panel_dev, 1) if r else piece
                out = piece if out is None else jnp.where(fold_group == r, piece, out)
            gath[me, pl.ds(at, step), :] = out
            return carry

        lax.fori_loop(0, fold // step, folded, 0)

    block = 512

    def take(tile):
        lanes = pl.ds(pl.multiple_of(tile * LANES, LANES), LANES)

        def store_panel(j, at, value):
            panel_ref[pl.ds(j * fold + at.start, at.size), lanes] = value

        regroup(lambda r, at: gath[tile * folds + r, at, :], store_panel, folds, fold)

        def product(k, total):
            at = pl.ds(pl.multiple_of(k * block, block), block)
            return total + dot(own_ref[at, :], panel_ref[at, lanes], (0, 0))

        part[:, lanes] = lax.fori_loop(
            0, points // block, product, jnp.zeros((LANES, LANES), jnp.float32)
        )

    if folds == 2:
        gather_orb(orbs, me, gath, g_send, g_recv, gs_send, gs_recv, take, during)
    else:
        gather_orb(orbs, me, gath, g_send, g_recv, gs_send, gs_recv)

        def each(tile, carry):
            take(tile)
            return carry

        lax.fori_loop(0, PANEL // LANES, each, 0)

    top, rest = part.at[:panel_dev], part.at[panel_dev:]
    top_land, rest_land = part_land.at[:, :panel_dev], part_land.at[:, panel_dev:]
    exchange(slabs, here, c_send, c_recv, lambda there: top, top_land)
    exchange(slabs, here, d_send, d_recv, lambda there: rest, rest_land)
    part_land[here] = part[...]
    points_all = points * slabs

    def summed(view):
        total = view[0]
        for s in range(1, slabs):
            total += view[s]
        return total / points_all

    wait_exchange(slabs, here, c_send, c_recv, lambda there: top, top_land)
    rows_land[me] = summed(top_land)
    gather_orb(orbs, me, rows_land, h_send, h_recv, hs_send, hs_recv)
    wait_exchange(slabs, here, d_send, d_recv, lambda there: rest, rest_land)
    cross_ref[:panel_dev, :] = jnp.zeros((panel_dev, PANEL), jnp.float32)
    cross_ref[panel_dev:, :] = summed(rest_land)
    for o in range(orbs):
        gram_ref[o * panel_dev : (o + 1) * panel_dev, :] = rows_land[o]


def block_inverse(a):
    n = LANES
    tiles = n // 8
    rows = lax.broadcasted_iota(jnp.int32, (8, n), 0)
    cols = lax.broadcasted_iota(jnp.int32, (8, n), 1)
    work = [a[8 * t : 8 * t + 8] for t in range(tiles)]
    unit = [jnp.where(rows + 8 * t == cols, 1.0, 0.0).astype(jnp.float32) for t in range(tiles)]
    for t0 in range(tiles):
        base = 8 * t0
        columns = [jnp.broadcast_to(work[t0][:, base + k : base + k + 1], (8, n)) for k in range(8)]
        small = {
            (i, k): jnp.broadcast_to(columns[k][i : i + 1], (8, n)) for i in range(8) for k in range(i + 1)
        }
        lower, scales = {}, []
        for j in range(8):
            scales.append(1.0 / small[j, j])
            for i in range(j + 1, 8):
                lower[i, j] = small[i, j] * scales[j]
            for i in range(j + 1, 8):
                for k in range(j + 1, i + 1):
                    small[i, k] = small[i, k] - lower[i, j] * small[k, j]
        turned = {}
        for j in range(8):
            for i in range(j + 1, 8):
                value = lower[i, j]
                for k in range(j + 1, i):
                    value = value + lower[i, k] * turned[k, j]
                turned[i, j] = -value
        a_row, u_row = work[t0], unit[t0]
        a_new, u_new = a_row, u_row
        for k in range(7):
            weight = jnp.zeros((8, n), jnp.float32)
            for i in range(k + 1, 8):
                weight = jnp.where(rows == i, turned[i, k], weight)
            a_new = a_new + weight * jnp.broadcast_to(a_row[k : k + 1], (8, n))
            u_new = u_new + weight * jnp.broadcast_to(u_row[k : k + 1], (8, n))
        work[t0], unit[t0] = a_new, u_new
        if t0 == tiles - 1:
            break
        a_out = u_out = None
        for i in range(8):
            weight = jnp.where(rows == i, scales[i], 0.0)
            for k in range(i):
                weight = jnp.where(rows == k, turned[i, k] * scales[i], weight)
            a_term = weight * jnp.broadcast_to(a_new[i : i + 1], (8, n))
            u_term = weight * jnp.broadcast_to(u_new[i : i + 1], (8, n))
            a_out = a_term if a_out is None else a_out + a_term
            u_out = u_term if u_out is None else u_out + u_term
        a_rows = [jnp.broadcast_to(a_out[k : k + 1], (8, n)) for k in range(8)]
        u_rows = [jnp.broadcast_to(u_out[k : k + 1], (8, n)) for k in range(8)]
        for t in range(t0 + 1, tiles):
            before = work[t]
            for k in range(8):
                column = jnp.broadcast_to(before[:, base + k : base + k + 1], (8, n))
                work[t] = work[t] - column * a_rows[k]
                unit[t] = unit[t] - column * u_rows[k]
    out = []
    for t in range(tiles):
        pivots = jnp.sum(jnp.where(rows + 8 * t == cols, work[t], 0.0), axis=1, keepdims=True)
        out.append(unit[t] * (1.0 / jnp.sqrt(pivots)))
    return jnp.concatenate(out, axis=0)


def solve_kernel(orbs, own_ref, panel_ref, gram_ref, cross_ref, out_ref, work, inverse, weights):
    panel_dev = PANEL // orbs
    me = lax.axis_index("orb")
    n = LANES
    blocks = PANEL // n
    work[...] = gram_ref[...]
    inverse[...] = jnp.zeros_like(inverse)

    def factor(b, carry):
        at = pl.multiple_of(b * n, n)
        diag = block_inverse(work[pl.ds(at, n), pl.ds(at, n)])
        inverse[pl.ds(at, n), pl.ds(at, n)] = diag
        for i in range(1, blocks):
            @pl.when(i > b)
            def _():
                work[i * n : (i + 1) * n, pl.ds(at, n)] = dot(
                    work[i * n : (i + 1) * n, pl.ds(at, n)], diag, (1, 1)
                )
        for i in range(1, blocks):
            @pl.when(i > b)
            def _():
                left = work[i * n : (i + 1) * n, pl.ds(at, n)]
                for k in range(1, i + 1):
                    @pl.when(k > b)
                    def _():
                        right = work[k * n : (k + 1) * n, pl.ds(at, n)]
                        work[i * n : (i + 1) * n, k * n : (k + 1) * n] -= dot(left, right, (1, 1))
        return carry

    lax.fori_loop(0, blocks, factor, 0)
    for i in range(1, blocks):
        span = i * n
        inner = dot(work[i * n : (i + 1) * n, :span], inverse[:span, :span], (1, 0))
        inverse[i * n : (i + 1) * n, :span] = -dot(
            inverse[i * n : (i + 1) * n, i * n : (i + 1) * n], inner, (1, 0)
        )

    middle = dot(cross_ref[...], inverse[...], (1, 1))
    weights[...] = -dot(middle, inverse[...], (1, 0))
    weights[:panel_dev, :] = inverse[pl.ds(pl.multiple_of(me * panel_dev, panel_dev), panel_dev), :]
    points = own_ref.shape[0]
    block = 256
    lanes = lax.broadcasted_iota(jnp.int32, (block, LANES), 1)

    def final(k, carry):
        at = pl.ds(pl.multiple_of(k * block, block), block)
        kept = jnp.where(lanes < panel_dev, 0.0, own_ref[at, :])
        out_ref[at, :] = kept + dot(panel_ref[at, :], weights[...], (1, 1))
        return carry

    lax.fori_loop(0, points // block, final, 0)


def per_device(slabs, orbs, orbitals, potential):
    planes, rows_y, rows_z, columns = orbitals.shape
    points = planes * rows_y * rows_z
    panel_dev = PANEL // orbs
    folds = LANES // panel_dev
    thin = points // LANES
    f32 = jnp.float32
    vmem = pl.BlockSpec(memory_space=pltpu.VMEM)
    dma = pltpu.SemaphoreType.DMA
    steps = max(orbs // 2 - 1, 1)
    split = folds == 2 and planes == slabs and rows_y // 2 >= REACH and steps >= 2
    flat = orbitals.reshape(points, columns)
    own, panel, gram, cross = pl.pallas_call(
        functools.partial(filter_kernel, slabs, orbs, (planes, rows_y, rows_z), split),
        out_shape=[
            jax.ShapeDtypeStruct((points, LANES), f32),
            jax.ShapeDtypeStruct((points, PANEL), f32),
            jax.ShapeDtypeStruct((PANEL, PANEL), f32),
            jax.ShapeDtypeStruct((LANES, PANEL), f32),
        ],
        in_specs=[vmem] * 2,
        out_specs=[vmem] * 4,
        scratch_shapes=[pltpu.VMEM((slabs, points // slabs, LANES), f32)] * 4
        + [
            pltpu.VMEM((slabs, thin, LANES), f32),
            pltpu.VMEM(((9 if split else 6) * points // 2, LANES), f32),
            pltpu.VMEM(((9 if split else 6) * points // 2, LANES), f32),
            pltpu.VMEM((points, LANES), f32),
            pltpu.VMEM((orbs, points // folds, LANES), f32),
            pltpu.VMEM((LANES, PANEL), f32),
            pltpu.VMEM((slabs, LANES, PANEL), f32),
            pltpu.VMEM((orbs, panel_dev, PANEL), f32),
        ]
        + [dma((slabs,))] * 14
        + [dma((2, steps))] * 2 + [dma((2 * steps + 1,))] * 2
        + [dma((2, steps))] * 2 + [dma((2 * steps + 1,))] * 2,
        compiler_params=pltpu.CompilerParams(
            collective_id=0, has_side_effects=True, vmem_limit_bytes=48 << 20
        ),
    )(flat, potential.reshape(LANES, thin).T)
    out = pl.pallas_call(
        functools.partial(solve_kernel, orbs),
        out_shape=jax.ShapeDtypeStruct((points, LANES), f32),
        in_specs=[vmem] * 4,
        out_specs=vmem,
        scratch_shapes=[
            pltpu.VMEM((PANEL, PANEL), f32),
            pltpu.VMEM((PANEL, PANEL), f32),
            pltpu.VMEM((LANES, PANEL), f32),
        ],
        compiler_params=pltpu.CompilerParams(vmem_limit_bytes=32 << 20),
    )(own, panel, gram, cross)
    return out.reshape(planes, rows_y, rows_z, columns)


def solution(mesh):
    placed = (P("space", None, None, "orb"), P("space", None, None))
    return jax.shard_map(
        functools.partial(per_device, mesh.shape["space"], mesh.shape["orb"]),
        mesh=mesh,
        in_specs=placed,
        out_specs=P("space", None, None, "orb"),
        check_vma=False,
    )
```

```python
import functools

import jax
import jax.numpy as jnp
from jax import lax
from jax.experimental import pallas as pl
from jax.experimental.pallas import tpu as pltpu
from jax.sharding import PartitionSpec as P

PANEL = 512
DEGREE = 4

STENCIL = (-205.0 / 72.0, 8.0 / 5.0, -1.0 / 5.0, 8.0 / 315.0, -1.0 / 560.0)
SHIFT_MID = 7.25
HALF_WIDTH = 4.75
LANES = 128
REACH = 4
MESH = pl.DeviceIdType.MESH
HIGHEST = lax.Precision.HIGHEST


def dot(a, b, dims):
    return lax.dot_general(
        a, b, ((dims[:1], dims[1:]), ((), ())), precision=HIGHEST, preferred_element_type=jnp.float32
    )


def regroup(load, store, count, rows):
    width = LANES // count
    step = min(rows, max(8, 128 // count))
    group = lax.broadcasted_iota(jnp.int32, (step, LANES), 1) // width

    def body(block, carry):
        here = pl.ds(pl.multiple_of(block * step, step), step)
        parts = [load(r, here) for r in range(count)]
        for j in range(count):
            out = None
            for r in range(count):
                turn = ((r - j) * width) % LANES
                piece = pltpu.roll(parts[r], turn, 1) if turn else parts[r]
                out = piece if out is None else jnp.where(group == r, piece, out)
            store(j, here, out)
        return carry

    lax.fori_loop(0, rows // step, body, 0)


def exchange(slots, here, send_sem, recv_sem, send, land):
    copies = []
    for hop in range(1, slots):
        there = lax.rem(here + hop, slots)
        copy = pltpu.make_async_remote_copy(
            src_ref=send(there),
            dst_ref=land.at[here],
            send_sem=send_sem.at[hop],
            recv_sem=recv_sem.at[hop],
            device_id={"space": there},
            device_id_type=MESH,
        )
        copy.start()
        copies.append(copy)
    return copies


def wait_exchange(slots, here, send_sem, recv_sem, send, land):
    for hop in range(1, slots):
        there = lax.rem(here + hop, slots)
        source = lax.rem(here + slots - hop, slots)
        pltpu.make_async_remote_copy(
            src_ref=send(there),
            dst_ref=land.at[source],
            send_sem=send_sem.at[hop],
            recv_sem=recv_sem.at[hop],
            device_id={"space": there},
            device_id_type=MESH,
        ).wait()


def gather_orb(count, me, buf, send_sem, recv_sem, side_send, side_recv, arrived=lambda chip: None, during=None):
    chips = count // 2
    chip, core = me // 2, lax.rem(me, 2)
    partner = chip * 2 + (1 - core)

    def along(origin, to, way, step):
        slot = buf.at[origin * 2 + core]
        return pltpu.make_async_remote_copy(
            src_ref=slot,
            dst_ref=slot,
            send_sem=send_sem.at[way, step],
            recv_sem=recv_sem.at[way, step],
            device_id={"orb": to * 2 + core},
            device_id_type=MESH,
        )

    def across(origin, side, index):
        slot = buf.at[origin * 2 + side]
        return pltpu.make_async_remote_copy(
            src_ref=slot,
            dst_ref=slot,
            send_sem=side_send.at[index],
            recv_sem=side_recv.at[index],
            device_id={"orb": partner},
            device_id_type=MESH,
        )

    steps = chips - 1

    def finish(step):
        @pl.when(chip - 1 - step >= 0)
        def _():
            across(chip - 1 - step, 1 - core, 1 + step).wait_recv()
            arrived(chip - 1 - step)

        @pl.when(chip + 1 + step < chips)
        def _():
            across(chip + 1 + step, 1 - core, 1 + steps + step).wait_recv()
            arrived(chip + 1 + step)

    for step in range(steps):
        @pl.when((chip - step >= 0) & (chip + 1 < chips))
        def _():
            along(chip - step, chip + 1, 0, step).start()

        @pl.when((chip + step < chips) & (chip - 1 >= 0))
        def _():
            along(chip + step, chip - 1, 1, step).start()

        if step == 0:
            across(chip, core, 0).start()
            if during:
                during[0]()
        if step == (1 if during else 0):
            if during:
                during[1]()
            across(chip, 1 - core, 0).wait_recv()
            arrived(chip)
        if step:
            finish(step - 1)

        @pl.when(chip - 1 - step >= 0)
        def _():
            along(chip - 1 - step, chip, 0, step).wait_recv()
            across(chip - 1 - step, core, 1 + step).start()

        @pl.when(chip + 1 + step < chips)
        def _():
            along(chip + 1 + step, chip, 1, step).wait_recv()
            across(chip + 1 + step, core, 1 + steps + step).start()

    finish(steps - 1)
    across(chip, core, 0).wait_send()
    for step in range(steps):
        @pl.when((chip - step >= 0) & (chip + 1 < chips))
        def _():
            along(chip - step, chip + 1, 0, step).wait_send()

        @pl.when((chip + step < chips) & (chip - 1 >= 0))
        def _():
            along(chip + step, chip - 1, 1, step).wait_send()

        @pl.when(chip - 1 - step >= 0)
        def _():
            across(chip - 1 - step, core, 1 + step).wait_send()

        @pl.when(chip + 1 + step < chips)
        def _():
            across(chip + 1 + step, core, 1 + steps + step).wait_send()


def split_filter(
    slabs, shape, here, me, x_ref, pot_ref, own_ref, pack, land, pack_back, land_back, pot_land,
    wide_a, wide_b, level, gath, out_sems, pot_sems, back_sems,
):
    planes, rows_y, rows_z = shape
    points = planes * rows_y * rows_z
    slots = 2 * slabs
    width = LANES // slots
    rows = points // slots
    plane = 3 * rows
    thin = points // LANES
    step = 16
    slot = lax.broadcasted_iota(jnp.int32, (step, LANES), 1) // width

    def merge(parts):
        out = None
        for u, (value, v) in enumerate(parts):
            turn = ((u - v) * width) % LANES
            value = pltpu.roll(value, turn, 1) if turn else value
            out = value if out is None else jnp.where(slot == u, value, out)
        return out

    def over(body):
        def one(block, carry):
            body(pl.multiple_of(block * step, step))
            return carry

        lax.fori_loop(0, rows // step, one, 0)

    def half(buf, h):
        return buf.at[:, h * rows : (h + 1) * rows]

    def send(buf, landing, h, sems):
        exchange(slabs, here, *sems[h], lambda there: half(buf, h).at[there], half(landing, h))
        landing[here, h * rows : (h + 1) * rows] = buf[here, h * rows : (h + 1) * rows]

    def wait(buf, landing, h, sems):
        wait_exchange(slabs, here, *sems[h], lambda there: half(buf, h).at[there], half(landing, h))

    def pack_half(h):
        def body(at):
            parts = [x_ref[pl.ds(q * rows + at, step), :] for q in range(slots)]
            for j in range(slabs):
                pack[j, pl.ds(h * rows + at, step), :] = merge([(part, h * slabs + j) for part in parts])

        over(body)
        send(pack, land, h, out_sems)

    def put(target, p, row, value):
        odd = lax.rem(lax.broadcasted_iota(jnp.int32, value.shape, 1) // width, 2)
        size = value.shape[0]
        swapped = jnp.where(odd == 0, pltpu.roll(value, LANES - width, 1), pltpu.roll(value, width, 1))
        target[pl.ds((planes + p) * plane + rows + row, size), :] = value
        target[pl.ds((planes + p) * plane + row, size), :] = swapped
        target[pl.ds((planes + p) * plane + 2 * rows + row, size), :] = swapped
        target[pl.ds(p * plane + rows + row, size), :] = pltpu.roll(value, 2 * width, 1)
        target[pl.ds((2 * planes + p) * plane + rows + row, size), :] = pltpu.roll(value, LANES - 2 * width, 1)

    taps = [-0.5 * c / HALF_WIDTH for c in STENCIL]

    def sweep(source, target, first):
        def body(y, carry):
            for p in range(planes):
                def line(q, yy):
                    row = pl.multiple_of((planes + q) * plane + rows + yy * rows_z, rows_z)
                    return source[pl.ds(row, rows_z), :]

                row = pl.multiple_of(y * rows_z, rows_z)
                centre = line(p, y)
                total = level[pl.ds(p * rows + row, rows_z), :] * centre
                for m in range(1, REACH + 1):
                    near = line(p + m, y) + line(p - m, y) + line(p, y + m) + line(p, y - m)
                    near += pltpu.roll(centre, m, 0) + pltpu.roll(centre, rows_z - m, 0)
                    total += taps[m] * near
                if not first:
                    total = 2.0 * total - target[pl.ds((planes + p) * plane + rows + row, rows_z), :]
                put(target, p, row, total)
            return carry

        lax.fori_loop(0, rows_y // 2, body, 0)

    def filter_half(h):
        wait(pack, land, h, out_sems)

        def unpack(at):
            parts = [land[i, pl.ds(h * rows + at, step), :] for i in range(slabs)]
            for p in range(planes):
                put(wide_a, p, at, merge([(parts[u // 2], 2 * p + u % 2) for u in range(slots)]))

        over(unpack)
        sweep(wide_a, wide_b, True)
        source, target = wide_b, wide_a
        for _ in range(DEGREE - 1):
            sweep(source, target, False)
            source, target = target, source

        def body(at):
            parts = [source[pl.ds((planes + p) * plane + rows + at, step), :] for p in range(planes)]
            for i in range(slabs):
                pack_back[i, pl.ds(h * rows + at, step), :] = merge(
                    [(parts[q // 2], 2 * i + q % 2) for q in range(slots)]
                )

        over(body)
        send(pack_back, land_back, h, back_sems)

    pack_half(0)
    pack_half(1)
    pot_land[here] = pot_ref[...]
    wait_exchange(slabs, here, *pot_sems, lambda there: pot_ref, pot_land)
    lane_slot = lax.broadcasted_iota(jnp.int32, (thin, LANES), 1) // width
    fields = [pot_land[s] for s in range(slabs)]
    pieces = rows // thin
    for p in range(planes):
        for e in range(pieces):
            value = None
            for u in range(slots):
                l = (2 * p + u % 2) * pieces + e
                spread = jnp.broadcast_to(fields[u // 2][:, l : l + 1], (thin, LANES))
                value = spread if value is None else jnp.where(lane_slot == u, spread, value)
            level[pl.ds(p * rows + e * thin, thin), :] = (
                value - (SHIFT_MID + 1.5 * STENCIL[0])
            ) * (1.0 / HALF_WIDTH)

    filter_half(0)
    wait(pack_back, land_back, 0, back_sems)

    def fold_own(at):
        parts = [land_back[j, pl.ds(at, step), :] for j in range(slabs)]
        for k in range(slabs):
            gath[me, pl.ds(k * rows + at, step), :] = merge(
                [(parts[u % slabs], (u // slabs) * slabs + k) for u in range(slots)]
            )

    over(fold_own)

    def finish():
        wait(pack_back, land_back, 1, back_sems)

        def body(at):
            parts = [
                land_back[u % slabs, pl.ds((u // slabs) * rows + at, step), :] for u in range(slots)
            ]
            for q in range(slots):
                own_ref[pl.ds(q * rows + at, step), :] = merge([(part, q) for part in parts])

        over(body)

    return (lambda: filter_half(1)), finish


def filter_kernel(
    slabs, orbs, shape, split,
    x_ref, pot_ref, own_ref, panel_ref, gram_ref, cross_ref,
    pack, land, pack_back, land_back, pot_land, wide_a, wide_b, level, gath, part, part_land, rows_land,
    a_send, a_recv, p_send, p_recv, b_send, b_recv, c_send, c_recv, d_send, d_recv, e_send, e_recv, f_send, f_recv,
    g_send, g_recv, gs_send, gs_recv, h_send, h_recv, hs_send, hs_recv,
):
    planes, rows_y, rows_z = shape
    points = planes * rows_y * rows_z
    here, me = lax.axis_index("space"), lax.axis_index("orb")
    chunk = points // slabs
    width = LANES // slabs

    barrier = pltpu.get_barrier_semaphore()
    for hop in range(1, slabs):
        pl.semaphore_signal(
            barrier, inc=1, device_id={"space": lax.rem(here + hop, slabs)}, device_id_type=MESH
        )
    for hop in range(1, orbs):
        pl.semaphore_signal(
            barrier, inc=1, device_id={"orb": lax.rem(me + hop, orbs)}, device_id_type=MESH
        )
    pl.semaphore_wait(barrier, slabs - 1 + orbs - 1)

    exchange(slabs, here, p_send, p_recv, lambda there: pot_ref, pot_land)

    panel_dev = PANEL // orbs
    folds = LANES // panel_dev
    fold = points // folds
    during = None
    if split:
        during = split_filter(
            slabs, shape, here, me, x_ref, pot_ref, own_ref, pack, land, pack_back, land_back, pot_land,
            wide_a, wide_b, level, gath,
            ((a_send, a_recv), (e_send, e_recv)), (p_send, p_recv), ((b_send, b_recv), (f_send, f_recv)),
        )
    else:
        def store_pack(j, at, value):
            pack[j, at, :] = value

        regroup(lambda r, at: x_ref[pl.ds(r * chunk + at.start, at.size), :], store_pack, slabs, chunk)
        exchange(slabs, here, a_send, a_recv, lambda there: pack.at[there], land)
        land[here] = pack[here]
        pot_land[here] = pot_ref[...]
        wait_exchange(slabs, here, p_send, p_recv, lambda there: pot_ref, pot_land)

        thin = points // LANES
        lane_group = lax.broadcasted_iota(jnp.int32, (thin, LANES), 1) // width
        fields = [pot_land[s] for s in range(slabs)]
        for l in range(LANES):
            value = None
            for s in range(slabs):
                spread = jnp.broadcast_to(fields[s][:, l : l + 1], (thin, LANES))
                value = spread if value is None else jnp.where(lane_group == s, spread, value)
            level[pl.ds(l * thin, thin), :] = (value - (SHIFT_MID + 1.5 * STENCIL[0])) * (1.0 / HALF_WIDTH)

        wait_exchange(slabs, here, a_send, a_recv, lambda there: pack.at[there], land)

        def put(target, row, value):
            target[pl.ds(points + row, value.shape[0]), :] = value
            target[pl.ds(row, value.shape[0]), :] = pltpu.roll(value, width, 1)
            target[pl.ds(2 * points + row, value.shape[0]), :] = pltpu.roll(value, LANES - width, 1)

        regroup(
            lambda r, at: land[r, at, :],
            lambda j, at, value: put(wide_a, j * chunk + at.start, value),
            slabs, chunk,
        )

        plane = rows_y * rows_z
        taps = [-0.5 * c / HALF_WIDTH for c in STENCIL]

        def sweep(source, target, first):
            def body(y, carry):
                for p in range(planes):
                    def line(q, yy):
                        return source[pl.ds(pl.multiple_of(points + q * plane + yy * rows_z, rows_z), rows_z), :]

                    row = pl.multiple_of(p * plane + y * rows_z, rows_z)
                    centre = line(p, y)
                    total = level[pl.ds(row, rows_z), :] * centre
                    for m in range(1, REACH + 1):
                        near = line(p + m, y) + line(p - m, y)
                        near += line(p, lax.rem(y + m, rows_y)) + line(p, lax.rem(y + rows_y - m, rows_y))
                        near += pltpu.roll(centre, m, 0) + pltpu.roll(centre, rows_z - m, 0)
                        total += taps[m] * near
                    if not first:
                        before = target[pl.ds(pl.multiple_of(points + row, rows_z), rows_z), :]
                        total = 2.0 * total - before
                    put(target, row, total)
                return carry

            lax.fori_loop(0, rows_y, body, 0)

        sweep(wide_a, wide_b, True)
        source, target = wide_b, wide_a
        for _ in range(DEGREE - 1):
            sweep(source, target, False)
            source, target = target, source

        def store_back(j, at, value):
            pack_back[j, at, :] = value

        regroup(
            lambda r, at: source[pl.ds(points + r * chunk + at.start, at.size), :], store_back, slabs, chunk
        )
        exchange(slabs, here, b_send, b_recv, lambda there: pack_back.at[there], land_back)
        land_back[here] = pack_back[here]
        wait_exchange(slabs, here, b_send, b_recv, lambda there: pack_back.at[there], land_back)

        def store_own(j, at, value):
            own_ref[pl.ds(j * chunk + at.start, at.size), :] = value

        regroup(lambda r, at: land_back[r, at, :], store_own, slabs, chunk)

        step = min(fold, 32)
        fold_group = lax.broadcasted_iota(jnp.int32, (step, LANES), 1) // panel_dev

        def folded(block, carry):
            at = pl.multiple_of(block * step, step)
            out = None
            for r in range(folds):
                piece = own_ref[pl.ds(r * fold + at, step), :]
                piece = pltpu.roll(piece, r * panel_dev, 1) if r else piece
                out = piece if out is None else jnp.where(fold_group == r, piece, out)
            gath[me, pl.ds(at, step), :] = out
            return carry

        lax.fori_loop(0, fold // step, folded, 0)

    block = 512

    def take(tile):
        lanes = pl.ds(pl.multiple_of(tile * LANES, LANES), LANES)

        def store_panel(j, at, value):
            panel_ref[pl.ds(j * fold + at.start, at.size), lanes] = value

        regroup(lambda r, at: gath[tile * folds + r, at, :], store_panel, folds, fold)

        def product(k, total):
            at = pl.ds(pl.multiple_of(k * block, block), block)
            return total + dot(own_ref[at, :], panel_ref[at, lanes], (0, 0))

        part[:, lanes] = lax.fori_loop(
            0, points // block, product, jnp.zeros((LANES, LANES), jnp.float32)
        )

    if folds == 2:
        gather_orb(orbs, me, gath, g_send, g_recv, gs_send, gs_recv, take, during)
    else:
        gather_orb(orbs, me, gath, g_send, g_recv, gs_send, gs_recv)

        def each(tile, carry):
            take(tile)
            return carry

        lax.fori_loop(0, PANEL // LANES, each, 0)

    top, rest = part.at[:panel_dev], part.at[panel_dev:]
    top_land, rest_land = part_land.at[:, :panel_dev], part_land.at[:, panel_dev:]
    exchange(slabs, here, c_send, c_recv, lambda there: top, top_land)
    exchange(slabs, here, d_send, d_recv, lambda there: rest, rest_land)
    part_land[here] = part[...]
    points_all = points * slabs

    def summed(view):
        total = view[0]
        for s in range(1, slabs):
            total += view[s]
        return total / points_all

    wait_exchange(slabs, here, c_send, c_recv, lambda there: top, top_land)
    rows_land[me] = summed(top_land)
    gather_orb(orbs, me, rows_land, h_send, h_recv, hs_send, hs_recv)
    wait_exchange(slabs, here, d_send, d_recv, lambda there: rest, rest_land)
    cross_ref[:panel_dev, :] = jnp.zeros((panel_dev, PANEL), jnp.float32)
    cross_ref[panel_dev:, :] = summed(rest_land)
    for o in range(orbs):
        gram_ref[o * panel_dev : (o + 1) * panel_dev, :] = rows_land[o]


def block_inverse(a):
    n = LANES
    tiles = n // 8
    rows = lax.broadcasted_iota(jnp.int32, (8, n), 0)
    cols = lax.broadcasted_iota(jnp.int32, (8, n), 1)
    work = [a[8 * t : 8 * t + 8] for t in range(tiles)]
    unit = [jnp.where(rows + 8 * t == cols, 1.0, 0.0).astype(jnp.float32) for t in range(tiles)]
    for t0 in range(tiles):
        base = 8 * t0
        columns = [jnp.broadcast_to(work[t0][:, base + k : base + k + 1], (8, n)) for k in range(8)]
        small = {
            (i, k): jnp.broadcast_to(columns[k][i : i + 1], (8, n)) for i in range(8) for k in range(i + 1)
        }
        lower, scales = {}, []
        for j in range(8):
            scales.append(1.0 / small[j, j])
            for i in range(j + 1, 8):
                lower[i, j] = small[i, j] * scales[j]
            for i in range(j + 1, 8):
                for k in range(j + 1, i + 1):
                    small[i, k] = small[i, k] - lower[i, j] * small[k, j]
        turned = {}
        for j in range(8):
            for i in range(j + 1, 8):
                value = lower[i, j]
                for k in range(j + 1, i):
                    value = value + lower[i, k] * turned[k, j]
                turned[i, j] = -value
        a_row, u_row = work[t0], unit[t0]
        a_new, u_new = a_row, u_row
        for k in range(7):
            weight = jnp.zeros((8, n), jnp.float32)
            for i in range(k + 1, 8):
                weight = jnp.where(rows == i, turned[i, k], weight)
            a_new = a_new + weight * jnp.broadcast_to(a_row[k : k + 1], (8, n))
            u_new = u_new + weight * jnp.broadcast_to(u_row[k : k + 1], (8, n))
        work[t0], unit[t0] = a_new, u_new
        if t0 == tiles - 1:
            break
        a_out = u_out = None
        for i in range(8):
            weight = jnp.where(rows == i, scales[i], 0.0)
            for k in range(i):
                weight = jnp.where(rows == k, turned[i, k] * scales[i], weight)
            a_term = weight * jnp.broadcast_to(a_new[i : i + 1], (8, n))
            u_term = weight * jnp.broadcast_to(u_new[i : i + 1], (8, n))
            a_out = a_term if a_out is None else a_out + a_term
            u_out = u_term if u_out is None else u_out + u_term
        a_rows = [jnp.broadcast_to(a_out[k : k + 1], (8, n)) for k in range(8)]
        u_rows = [jnp.broadcast_to(u_out[k : k + 1], (8, n)) for k in range(8)]
        for t in range(t0 + 1, tiles):
            before = work[t]
            for k in range(8):
                column = jnp.broadcast_to(before[:, base + k : base + k + 1], (8, n))
                work[t] = work[t] - column * a_rows[k]
                unit[t] = unit[t] - column * u_rows[k]
    out = []
    for t in range(tiles):
        pivots = jnp.sum(jnp.where(rows + 8 * t == cols, work[t], 0.0), axis=1, keepdims=True)
        out.append(unit[t] * (1.0 / jnp.sqrt(pivots)))
    return jnp.concatenate(out, axis=0)


def solve_kernel(orbs, own_ref, panel_ref, gram_ref, cross_ref, out_ref, work, inverse, weights):
    panel_dev = PANEL // orbs
    me = lax.axis_index("orb")
    n = LANES
    blocks = PANEL // n
    work[...] = gram_ref[...]
    inverse[...] = jnp.zeros_like(inverse)

    def factor(b, carry):
        at = pl.multiple_of(b * n, n)
        diag = block_inverse(work[pl.ds(at, n), pl.ds(at, n)])
        inverse[pl.ds(at, n), pl.ds(at, n)] = diag
        for i in range(1, blocks):
            @pl.when(i > b)
            def _():
                work[i * n : (i + 1) * n, pl.ds(at, n)] = dot(
                    work[i * n : (i + 1) * n, pl.ds(at, n)], diag, (1, 1)
                )
        for i in range(1, blocks):
            @pl.when(i > b)
            def _():
                left = work[i * n : (i + 1) * n, pl.ds(at, n)]
                for k in range(1, i + 1):
                    @pl.when(k > b)
                    def _():
                        right = work[k * n : (k + 1) * n, pl.ds(at, n)]
                        work[i * n : (i + 1) * n, k * n : (k + 1) * n] -= dot(left, right, (1, 1))
        return carry

    lax.fori_loop(0, blocks, factor, 0)
    for i in range(1, blocks):
        span = i * n
        inner = dot(work[i * n : (i + 1) * n, :span], inverse[:span, :span], (1, 0))
        inverse[i * n : (i + 1) * n, :span] = -dot(
            inverse[i * n : (i + 1) * n, i * n : (i + 1) * n], inner, (1, 0)
        )

    middle = dot(cross_ref[...], inverse[...], (1, 1))
    weights[...] = -dot(middle, inverse[...], (1, 0))
    weights[:panel_dev, :] = inverse[pl.ds(pl.multiple_of(me * panel_dev, panel_dev), panel_dev), :]
    points = own_ref.shape[0]
    block = 256
    lanes = lax.broadcasted_iota(jnp.int32, (block, LANES), 1)

    def final(k, carry):
        at = pl.ds(pl.multiple_of(k * block, block), block)
        kept = jnp.where(lanes < panel_dev, 0.0, own_ref[at, :])
        out_ref[at, :] = kept + dot(panel_ref[at, :], weights[...], (1, 1))
        return carry

    lax.fori_loop(0, points // block, final, 0)


def per_device(slabs, orbs, orbitals, potential):
    planes, rows_y, rows_z, columns = orbitals.shape
    points = planes * rows_y * rows_z
    panel_dev = PANEL // orbs
    folds = LANES // panel_dev
    thin = points // LANES
    f32 = jnp.float32
    vmem = pl.BlockSpec(memory_space=pltpu.VMEM)
    dma = pltpu.SemaphoreType.DMA
    steps = max(orbs // 2 - 1, 1)
    split = folds == 2 and planes == slabs and rows_y // 2 >= REACH and steps >= 2
    flat = orbitals.reshape(points, columns)
    own, panel, gram, cross = pl.pallas_call(
        functools.partial(filter_kernel, slabs, orbs, (planes, rows_y, rows_z), split),
        out_shape=[
            jax.ShapeDtypeStruct((points, LANES), f32),
            jax.ShapeDtypeStruct((points, PANEL), f32),
            jax.ShapeDtypeStruct((PANEL, PANEL), f32),
            jax.ShapeDtypeStruct((LANES, PANEL), f32),
        ],
        in_specs=[vmem] * 2,
        out_specs=[vmem] * 4,
        scratch_shapes=[pltpu.VMEM((slabs, points // slabs, LANES), f32)] * 4
        + [
            pltpu.VMEM((slabs, thin, LANES), f32),
            pltpu.VMEM(((9 if split else 6) * points // 2, LANES), f32),
            pltpu.VMEM(((9 if split else 6) * points // 2, LANES), f32),
            pltpu.VMEM((points, LANES), f32),
            pltpu.VMEM((orbs, points // folds, LANES), f32),
            pltpu.VMEM((LANES, PANEL), f32),
            pltpu.VMEM((slabs, LANES, PANEL), f32),
            pltpu.VMEM((orbs, panel_dev, PANEL), f32),
        ]
        + [dma((slabs,))] * 14
        + [dma((2, steps))] * 2 + [dma((2 * steps + 1,))] * 2
        + [dma((2, steps))] * 2 + [dma((2 * steps + 1,))] * 2,
        compiler_params=pltpu.CompilerParams(
            collective_id=0, has_side_effects=True, vmem_limit_bytes=32 << 20
        ),
    )(flat, potential.reshape(LANES, thin).T)
    out = pl.pallas_call(
        functools.partial(solve_kernel, orbs),
        out_shape=jax.ShapeDtypeStruct((points, LANES), f32),
        in_specs=[vmem] * 4,
        out_specs=vmem,
        scratch_shapes=[
            pltpu.VMEM((PANEL, PANEL), f32),
            pltpu.VMEM((PANEL, PANEL), f32),
            pltpu.VMEM((LANES, PANEL), f32),
        ],
        compiler_params=pltpu.CompilerParams(vmem_limit_bytes=32 << 20),
    )(own, panel, gram, cross)
    return out.reshape(planes, rows_y, rows_z, columns)


def solution(mesh):
    placed = (P("space", None, None, "orb"), P("space", None, None))
    return jax.shard_map(
        functools.partial(per_device, mesh.shape["space"], mesh.shape["orb"]),
        mesh=mesh,
        in_specs=placed,
        out_specs=P("space", None, None, "orb"),
        check_vma=False,
    )
```
